512 devices in a mesh: wide: 128 (over y, z, core), narrow: 4 (over x).
Axes of the slice: x: 4, y: 8, z: 8, core: 2. Of those that a mesh axis runs over, the one named last changes fastest.
Arguments:
- grad_out: bfloat16 [32768, 512], P('wide', 'narrow'), may hold values from -24 to 24
- relu_mask: int32 [32768, 512], P('wide', 'narrow'), may hold values 0 or 1
- features: bfloat16 [32768, 512], P('wide', 'narrow'), may hold values from -6 to 6
- hop1_mean: bfloat16 [32768, 512], P('wide', 'narrow'), may hold values from -6 to 6
- hop2_mean: bfloat16 [32768, 512], P('wide', 'narrow'), may hold values from -6 to 6
- w_self: bfloat16 [512, 512], P('narrow'), may hold values from -0.25 to 0.25
- w_hop1: bfloat16 [512, 512], P('narrow'), may hold values from -0.25 to 0.25
- w_hop2: bfloat16 [512, 512], P('narrow'), may hold values from -0.25 to 0.25
- norm: float32 [32768], P('wide'), may hold values from 0.05 to 1
- tile_src: int32 [16384], P('wide'), may hold values from 0 to 1
- tile_owner: int32 [16384], P('wide'), may hold values from 0 to 127, as said below
- tile_block: int32 [16384], P('wide'), may hold values from 0 to 1
- tile_cols: int32 [16384, 128, 8], P('wide'), may hold values from 0 to 127
Outputs:
- grad_features: bfloat16 [32768, 512], P('wide', 'narrow')
- weight_grads: float32 [3, 512, 512], P(None, 'wide', 'narrow')
The draws below stay inside these ranges and needn't reach their ends.
Inputs may be any that keep to these rules, and one draw needn't show every extreme that they name: `tile_owner`: the 128 tiles of one device name every device once as owner.
All inputs are finite; a program needn't handle non-finite values. No bound on the sum of `relu_mask` on one device may be relied on, other than what follows from the above.
Results may differ from the reference program's by a relative error of at most 0.0054.
Values may be sent and summed in bfloat16 or wider, within the bound.
No kernel may reach another device: no remote copies, remote signals or barrier semaphores. Data moves between devices by JAX's collectives and lax.ppermute only.
A program may use at most 64 MiB of HBM per device.

```python
import math
import jax
import jax.numpy as jnp
import numpy as np
from jax import lax

D = 512
BLOCK = 128
NNZ = 8
ROW_BLOCKS = 2
TILES = 128
NODES = 32768
TILES_ALL = 16384
N_WIDE = 128


def draw_tile_owner(key, part):
    row_keys = jax.random.split(jax.random.fold_in(key, 11), N_WIDE)
    orders = jax.vmap(lambda row_key: jax.random.permutation(row_key, N_WIDE))(row_keys)
    return orders.reshape(-1).astype(jnp.int32)


def touch_ends(drawn, key, smallest, largest):
    place = [jax.random.randint(jax.random.fold_in(key, axis), (), 0, length) for axis, length in enumerate(drawn.shape)]
    widest = drawn.shape.index(max(drawn.shape))
    beside = place[:widest] + [(place[widest] + 1) % drawn.shape[widest]] + place[widest + 1:]
    return drawn.at[tuple(place)].set(smallest).at[tuple(beside)].set(largest)


def raised(array, key, source, target, blocks, factor):
    def block_of(dim):
        return (jnp.arange(array.shape[dim]) // (array.shape[dim] // blocks)).reshape((-1,) + (1,) * (array.ndim - 1 - dim))

    first = jax.random.permutation(key, blocks)[block_of(target)]
    second = (block_of(target) + blocks // 2) % blocks
    return jnp.where((block_of(source) == first) | (block_of(source) == second), factor * array, array)


def steps_of(own_key, shape, cuts, low, high):
    def one(axis_at, shards_of):
        draws = jax.random.uniform(jax.random.fold_in(jax.random.fold_in(own_key, 6), axis_at), (shards_of,), jnp.float32, low / len(cuts), high / len(cuts))
        return jnp.repeat(jnp.exp(draws), shape[axis_at] // shards_of).reshape((-1,) + (1,) * (len(shape) - axis_at - 1))

    level = one(*cuts[0])
    for cut in cuts[1:]:
        level = level * one(*cut)
    return level


def cumulative_ranks(count, skew):
    portions = [(1 << 20) // math.isqrt(grade ** skew) + 1 for grade in range(1, count + 1)]
    deviation = 1 + sum(portions) // (1 << 30)
    return np.cumsum(np.array([max(1, weight // deviation) for weight in portions]))


def skewed_ids(stream_key, shape, amount, lean):
    table = cumulative_ranks(amount, lean)
    pick = jax.random.randint(jax.random.fold_in(stream_key, 1), shape, 0, int(table[amount - 1]))
    rank = jnp.searchsorted(jnp.asarray(table, jnp.int32), pick, side="right")
    return jax.random.permutation(jax.random.fold_in(stream_key, 2), amount)[rank].astype(jnp.int32)


def gaussian(own_key, dims, scale, limit, pieces=(), held_as=jnp.bfloat16):
    result = scale * jax.random.normal(own_key, dims, jnp.float32)
    if pieces:
        result = result * steps_of(own_key, dims, pieces, -0.22, 0.18)
    return jnp.clip(result, -limit, limit).astype(held_as)


def heavy_noise(rng, shape, width, bound, shards, heavy, held_as=jnp.bfloat16):
    result = width * jax.random.normal(rng, shape, jnp.float32)
    if shards:
        result = result * steps_of(rng, shape, shards, -0.22, 0.18)
    return jnp.clip(raised(result, jax.random.fold_in(rng, 3), *heavy), -bound, bound).astype(held_as)


def setup_inputs(seed: int = 0) -> dict:
    seeds = jax.random.split(jax.random.key(seed), 14)
    grad_out = heavy_noise(seeds[0], (NODES, D), 1.0, 24.0, ((0, 128), (1, 4)), (0, 1, 128, 5.5))
    relu_mask = touch_ends((jax.random.randint(seeds[1], (NODES, D), 0, 2) < 1).astype(jnp.int32), jax.random.fold_in(seeds[1], 1), 0, 1)
    features = gaussian(seeds[2], (NODES, D), 1.0, 6.0, ((0, 128), (1, 4)))
    hop1_mean = gaussian(seeds[3], (NODES, D), 1.0, 6.0, ((0, 128), (1, 4)))
    hop2_mean = gaussian(seeds[4], (NODES, D), 1.0, 6.0, ((0, 128), (1, 4)))
    w_self = gaussian(seeds[5], (D, D), D ** -0.5, 0.25, ((0, 4),))
    w_hop1 = gaussian(seeds[6], (D, D), D ** -0.5, 0.25, ((0, 4),))
    w_hop2 = gaussian(seeds[7], (D, D), D ** -0.5, 0.25, ((0, 4),))
    norm = jnp.clip(jnp.exp(math.log(1.0) - 2.9957323 * jax.random.uniform(seeds[8], (NODES,), jnp.float32) ** steps_of(seeds[8], (NODES,), ((0, 128),), -0.2, 0.2)), 0.05, 1.0)
    tile_src = touch_ends(jax.random.randint(seeds[9], (TILES_ALL,), 0, ROW_BLOCKS), jax.random.fold_in(seeds[9], 1), 0, ROW_BLOCKS - 1).astype(jnp.int32)
    tile_owner = draw_tile_owner(jax.random.fold_in(seeds[13], 71), 0)
    tile_block = touch_ends(skewed_ids(seeds[11], (TILES_ALL,), ROW_BLOCKS, 2), jax.random.fold_in(seeds[11], 3), 0, ROW_BLOCKS - 1).astype(jnp.int32)
    tile_cols = touch_ends(jax.random.randint(seeds[12], (TILES_ALL, BLOCK, NNZ), 0, BLOCK), jax.random.fold_in(seeds[12], 1), 0, BLOCK - 1).astype(jnp.int32)
    return {"grad_out": grad_out, "relu_mask": relu_mask, "features": features, "hop1_mean": hop1_mean, "hop2_mean": hop2_mean, "w_self": w_self, "w_hop1": w_hop1, "w_hop2": w_hop2, "norm": norm, "tile_src": tile_src, "tile_owner": tile_owner, "tile_block": tile_block, "tile_cols": tile_cols}


def tile_pattern(columns):
    positions = jnp.arange(BLOCK, dtype=jnp.int32)
    summed = jnp.zeros(columns.shape[:-1] + (BLOCK,), jnp.float32)
    for column in range(columns.shape[-1]):
        summed = summed + (columns[..., column, None] == positions).astype(jnp.float32)
    return summed


def transpose_hop(scaled, tile_src, tile_owner, tile_block, tile_cols):
    blocks = scaled.reshape(N_WIDE, ROW_BLOCKS, BLOCK, D)
    sources = tile_src.reshape(N_WIDE, TILES)
    owners = tile_owner.reshape(N_WIDE, TILES)
    targets = tile_block.reshape(N_WIDE, TILES)
    columns = tile_cols.reshape(N_WIDE, TILES, BLOCK, NNZ)

    def advance(accumulated, element):
        node_rows, source, owner, target, column = element
        picked = node_rows[source].astype(jnp.float32)
        products = jnp.einsum("trj,trd->tjd", tile_pattern(column), picked,
                              precision=lax.Precision.HIGHEST).astype(jnp.bfloat16)
        accumulated = accumulated.at[owner, target].add(products.astype(jnp.float32))
        return accumulated, None

    start = jnp.zeros((N_WIDE, ROW_BLOCKS, BLOCK, D), jnp.float32)
    accumulated, _ = lax.scan(advance, start, (blocks, sources, owners, targets, columns))
    return accumulated.reshape(NODES, D)


def reference(grad_out, relu_mask, features, hop1_mean, hop2_mean, w_self, w_hop1, w_hop2,
              norm, tile_src, tile_owner, tile_block, tile_cols):
    gated = grad_out * relu_mask.astype(jnp.bfloat16)
    weight_grads = jnp.stack([jnp.dot(gated.T, operand, preferred_element_type=jnp.float32)
                              for operand in (features, hop1_mean, hop2_mean)])
    row_scale = norm[:, None]
    scaled2 = (row_scale * jnp.dot(gated, w_hop2.T, preferred_element_type=jnp.float32)).astype(jnp.bfloat16)
    agg2 = transpose_hop(scaled2, tile_src, tile_owner, tile_block, tile_cols)
    scaled1 = (row_scale * (jnp.dot(gated, w_hop1.T, preferred_element_type=jnp.float32) + agg2)).astype(jnp.bfloat16)
    agg1 = transpose_hop(scaled1, tile_src, tile_owner, tile_block, tile_cols)
    grad_features = (jnp.dot(gated, w_self.T, preferred_element_type=jnp.float32) + agg1).astype(jnp.bfloat16)
    return grad_features, weight_grads
```

```python
import jax
import jax.numpy as jnp
from jax import lax
from jax.experimental import pallas as pl
from jax.experimental.pallas import tpu as pltpu
from jax.sharding import PartitionSpec as P

ROWS = 128
NNZ = 8
GROUP = 16


def route_kernel(owner_ref, src_ref, block_ref, cols_ref, out_ref):
    row = lax.broadcasted_iota(jnp.int32, (NNZ, ROWS), 0)

    def step(t, carry):
        cols = cols_ref[t]
        marks = jnp.where(row == 0, src_ref[t], jnp.where(row == 1, block_ref[t], 0))
        both = jnp.concatenate([cols, marks], axis=0).astype(jnp.float32)
        out_ref[owner_ref[t]] = both.astype(jnp.bfloat16)
        return carry

    lax.fori_loop(0, cols_ref.shape[0], step, 0)


def route(tile_owner, tile_src, tile_block, cols):
    tiles = cols.shape[0]
    return pl.pallas_call(
        route_kernel,
        out_shape=jax.ShapeDtypeStruct((tiles, 2 * NNZ, ROWS), jnp.bfloat16),
        grid_spec=pltpu.PrefetchScalarGridSpec(
            num_scalar_prefetch=3,
            grid=(1,),
            in_specs=[pl.BlockSpec(cols.shape, lambda i, *_: (0, 0, 0))],
            out_specs=pl.BlockSpec((tiles, 2 * NNZ, ROWS), lambda i, *_: (0, 0, 0)),
        ),
        cost_estimate=pl.CostEstimate(flops=1 << 20, bytes_accessed=1 << 20, transcendentals=0),
    )(tile_owner, tile_src, tile_block, cols)


def pattern_kernel(block_ref, cols_ref, out_ref):
    first = pl.program_id(0) * GROUP
    position = lax.broadcasted_iota(jnp.int32, (ROWS, ROWS), 0).astype(jnp.float32).astype(jnp.bfloat16)
    one = jnp.ones((ROWS, ROWS), jnp.bfloat16)
    zero = jnp.zeros((ROWS, ROWS), jnp.bfloat16)
    for d in range(GROUP):
        cols = cols_ref[d].astype(jnp.float32)
        count = zero
        for k in range(NNZ):
            line = jnp.broadcast_to(cols[k : k + 1, :], (ROWS, ROWS)).astype(jnp.bfloat16)
            count = count + jnp.where(line == position, one, zero)
        low = block_ref[first + d] == 0
        lanes = pl.ds(d * ROWS, ROWS)
        out_ref[0:ROWS, lanes] = jnp.where(low, count, zero)
        out_ref[ROWS : 2 * ROWS, lanes] = jnp.where(low, zero, count)


def build_pattern(block, arrived):
    tiles = arrived.shape[0]
    return pl.pallas_call(
        pattern_kernel,
        out_shape=jax.ShapeDtypeStruct((2 * ROWS, tiles * ROWS), jnp.bfloat16),
        grid_spec=pltpu.PrefetchScalarGridSpec(
            num_scalar_prefetch=1,
            grid=(tiles // GROUP,),
            in_specs=[pl.BlockSpec((GROUP, 2 * NNZ, ROWS), lambda i, *_: (i, 0, 0))],
            out_specs=pl.BlockSpec((2 * ROWS, GROUP * ROWS), lambda i, *_: (0, i)),
        ),
        cost_estimate=pl.CostEstimate(flops=1 << 26, bytes_accessed=9 << 20, transcendentals=0),
    )(block, arrived)


def hop_kernel(src_ref, rows_ref, pattern_ref, own_ref, scale_ref, out_ref, total_ref):
    step = pl.program_id(0)
    picked = []
    for d in range(GROUP):
        start = pl.multiple_of(d * 2 * ROWS + src_ref[step * GROUP + d] * ROWS, ROWS)
        picked.append(rows_ref[pl.ds(start, ROWS), :])
    part = jnp.dot(
        pattern_ref[...], jnp.concatenate(picked, axis=0), preferred_element_type=jnp.float32
    )

    @pl.when(step == 0)
    def _():
        total_ref[...] = own_ref[...] + part

    @pl.when(step > 0)
    def _():
        total_ref[...] += part

    @pl.when(step == pl.num_programs(0) - 1)
    def _():
        out_ref[...] = (scale_ref[...] * total_ref[...]).astype(jnp.bfloat16)


def hop(src, rows, pattern, own, scale):
    nodes, width = own.shape
    steps = rows.shape[0] // (GROUP * nodes)
    return pl.pallas_call(
        hop_kernel,
        out_shape=jax.ShapeDtypeStruct((nodes, width), jnp.bfloat16),
        grid_spec=pltpu.PrefetchScalarGridSpec(
            num_scalar_prefetch=1,
            grid=(steps,),
            in_specs=[
                pl.BlockSpec((GROUP * nodes, width), lambda i, *_: (i, 0)),
                pl.BlockSpec((nodes, GROUP * ROWS), lambda i, *_: (0, i)),
                pl.BlockSpec((nodes, width), lambda i, *_: (0, 0)),
                pl.BlockSpec((nodes, 1), lambda i, *_: (0, 0)),
            ],
            out_specs=pl.BlockSpec((nodes, width), lambda i, *_: (0, 0)),
            scratch_shapes=[pltpu.VMEM((nodes, width), jnp.float32)],
        ),
        cost_estimate=pl.CostEstimate(flops=1 << 30, bytes_accessed=17 << 20, transcendentals=0),
    )(src, rows, pattern, own, scale)


def on_device(
    grad_out,
    relu_mask,
    features,
    hop1_mean,
    hop2_mean,
    w_self,
    w_hop1,
    w_hop2,
    norm,
    tile_src,
    tile_owner,
    tile_block,
    tile_cols,
):
    gated = grad_out * relu_mask.astype(jnp.bfloat16)
    gated_full = lax.all_gather(gated, "narrow", axis=1, tiled=True)
    row_scale = norm[:, None]

    def project(weight):
        return lax.dot_general(
            gated_full, weight, (((1,), (1,)), ((), ())), preferred_element_type=jnp.float32
        )

    outgoing = route(tile_owner, tile_src, tile_block, jnp.swapaxes(tile_cols, 1, 2))
    scaled2 = (row_scale * project(w_hop2)).astype(jnp.bfloat16)
    scaled2, outgoing = lax.optimization_barrier((scaled2, outgoing))
    rows2 = lax.all_gather(scaled2, "wide", axis=0, tiled=True)
    arrived = lax.all_to_all(outgoing, "wide", split_axis=0, concat_axis=0, tiled=True)
    source = arrived[:, NNZ, 0].astype(jnp.int32)
    block = arrived[:, NNZ + 1, 0].astype(jnp.int32)
    pattern = build_pattern(block, arrived)
    scaled1 = hop(source, rows2, pattern, project(w_hop1), row_scale)
    partial_grads = jnp.stack(
        [
            jnp.einsum("ro,rd->od", gated_full, operand, preferred_element_type=jnp.float32)
            for operand in (features, hop1_mean, hop2_mean)
        ]
    )
    scaled1, partial_grads = lax.optimization_barrier((scaled1, partial_grads))
    rows1 = lax.all_gather(scaled1, "wide", axis=0, tiled=True)
    count = lax.axis_size("wide")
    kinds, outs, width = partial_grads.shape
    spread = lax.all_to_all(
        partial_grads.reshape(kinds, count, outs // count, width),
        "wide",
        split_axis=1,
        concat_axis=1,
        tiled=True,
    )
    weight_grads = spread.sum(axis=1)
    grad_features = hop(source, rows1, pattern, project(w_self), jnp.ones_like(row_scale))
    return (grad_features, weight_grads)


def solution(mesh):
    placed = (
        P("wide", "narrow"),
        P("wide", "narrow"),
        P("wide", "narrow"),
        P("wide", "narrow"),
        P("wide", "narrow"),
        P("narrow", None),
        P("narrow", None),
        P("narrow", None),
        P("wide"),
        P("wide"),
        P("wide"),
        P("wide"),
        P("wide", None, None),
    )
    return jax.shard_map(
        on_device,
        mesh=mesh,
        in_specs=placed,
        out_specs=(P("wide", "narrow"), P(None, "wide", "narrow")),
        check_vma=False,
    )
```

```python
import functools

import jax
import jax.numpy as jnp
import numpy as np
from jax import lax
from jax.experimental import pallas as pl
from jax.experimental.pallas import tpu as pltpu
from jax.sharding import PartitionSpec as P

ROWS = 128
NNZ = 8
GROUP = 16


def route_kernel(owner_ref, src_ref, block_ref, cols_ref, out_ref):
    row = lax.broadcasted_iota(jnp.int32, (NNZ, ROWS), 0)

    def step(t, carry):
        cols = cols_ref[t]
        marks = jnp.where(row == 0, src_ref[t], jnp.where(row == 1, block_ref[t], 0))
        both = jnp.concatenate([cols, marks], axis=0).astype(jnp.float32)
        out_ref[owner_ref[t]] = both.astype(jnp.bfloat16)
        return carry

    lax.fori_loop(0, cols_ref.shape[0], step, 0)


def route(tile_owner, tile_src, tile_block, cols):
    tiles = cols.shape[0]
    return pl.pallas_call(
        route_kernel,
        out_shape=jax.ShapeDtypeStruct((tiles, 2 * NNZ, ROWS), jnp.bfloat16),
        grid_spec=pltpu.PrefetchScalarGridSpec(
            num_scalar_prefetch=3,
            grid=(1,),
            in_specs=[pl.BlockSpec(cols.shape, lambda i, *_: (0, 0, 0))],
            out_specs=pl.BlockSpec((tiles, 2 * NNZ, ROWS), lambda i, *_: (0, 0, 0)),
        ),
        cost_estimate=pl.CostEstimate(flops=1 << 20, bytes_accessed=1 << 20, transcendentals=0),
    )(tile_owner, tile_src, tile_block, cols)


def pattern_kernel(order_ref, block_ref, cols_ref, out_ref):
    first = pl.program_id(0) * GROUP
    position = lax.broadcasted_iota(jnp.int32, (ROWS, ROWS), 0).astype(jnp.float32).astype(jnp.bfloat16)
    one = jnp.ones((ROWS, ROWS), jnp.bfloat16)
    zero = jnp.zeros((ROWS, ROWS), jnp.bfloat16)
    for slot in range(GROUP):
        device = order_ref[first + slot]
        cols = cols_ref[device].astype(jnp.float32)
        count = zero
        for k in range(NNZ):
            line = jnp.broadcast_to(cols[k : k + 1, :], (ROWS, ROWS)).astype(jnp.bfloat16)
            count = count + jnp.where(line == position, one, zero)
        low = block_ref[device] == 0
        lanes = pl.ds(slot * ROWS, ROWS)
        out_ref[0:ROWS, lanes] = jnp.where(low, count, zero)
        out_ref[ROWS : 2 * ROWS, lanes] = jnp.where(low, zero, count)


def build_pattern(order, block, arrived):
    tiles = arrived.shape[0]
    return pl.pallas_call(
        pattern_kernel,
        out_shape=jax.ShapeDtypeStruct((2 * ROWS, tiles * ROWS), jnp.bfloat16),
        grid_spec=pltpu.PrefetchScalarGridSpec(
            num_scalar_prefetch=2,
            grid=(tiles // GROUP,),
            in_specs=[pl.BlockSpec((tiles, 2 * NNZ, ROWS), lambda i, *_: (0, 0, 0))],
            out_specs=pl.BlockSpec((2 * ROWS, GROUP * ROWS), lambda i, *_: (0, i)),
        ),
        cost_estimate=pl.CostEstimate(flops=1 << 26, bytes_accessed=9 << 20, transcendentals=0),
    )(order, block, arrived)


def hop_kernel(natural, slots, order_ref, src_ref, pattern_ref, own_ref, scale_ref, *rest):
    pieces, (out_ref, total_ref, picked_ref, sems) = rest[:-4], rest[-4:]
    step = pl.program_id(0)

    def copy(piece, place, slot):
        start = pl.multiple_of((2 * place + src_ref[order_ref[slot]]) * ROWS, ROWS)
        return pltpu.make_async_copy(
            piece.at[pl.ds(start, ROWS), :], picked_ref.at[slot], sems.at[slot]
        )

    @pl.when(step == 0)
    def _():
        begin = 0
        for piece in pieces:
            held = piece.shape[0] // (2 * ROWS)

            def start(i, carry, piece=piece, begin=begin):
                slot = begin + i
                copy(piece, order_ref[slot] if natural else i, slot).start()
                return carry

            lax.fori_loop(0, held, start, 0)
            begin += held

    def wait(i, carry):
        slot = step * GROUP + i
        pltpu.make_async_copy(
            pieces[0].at[pl.ds(0, ROWS), :], picked_ref.at[slot], sems.at[slot]
        ).wait()
        return carry

    lax.fori_loop(0, GROUP, wait, 0)
    rows = picked_ref[pl.ds(step * GROUP, GROUP)].reshape(GROUP * ROWS, own_ref.shape[1])
    part = jnp.dot(pattern_ref[...], rows, preferred_element_type=jnp.float32)

    @pl.when(step == 0)
    def _():
        total_ref[...] = own_ref[...] + part

    @pl.when(step > 0)
    def _():
        total_ref[...] += part

    @pl.when(step == pl.num_programs(0) - 1)
    def _():
        out_ref[...] = (scale_ref[...] * total_ref[...]).astype(jnp.bfloat16)


def hop(order, src, pattern, own, scale, pieces, natural):
    nodes, width = own.shape
    slots = order.shape[0]
    return pl.pallas_call(
        functools.partial(hop_kernel, natural, slots),
        out_shape=jax.ShapeDtypeStruct((nodes, width), jnp.bfloat16),
        grid_spec=pltpu.PrefetchScalarGridSpec(
            num_scalar_prefetch=2,
            grid=(slots // GROUP,),
            in_specs=[
                pl.BlockSpec((nodes, GROUP * ROWS), lambda i, *_: (0, i)),
                pl.BlockSpec((nodes, width), lambda i, *_: (0, 0)),
                pl.BlockSpec((nodes, 1), lambda i, *_: (0, 0)),
            ]
            + [pl.BlockSpec(memory_space=pl.ANY)] * len(pieces),
            out_specs=pl.BlockSpec((nodes, width), lambda i, *_: (0, 0)),
            scratch_shapes=[
                pltpu.VMEM((nodes, width), jnp.float32),
                pltpu.VMEM((slots, ROWS, width), jnp.bfloat16),
                pltpu.SemaphoreType.DMA((slots,)),
            ],
        ),
        compiler_params=pltpu.CompilerParams(vmem_limit_bytes=(48 if natural else 12) << 20),
        cost_estimate=pl.CostEstimate(flops=1 << 30, bytes_accessed=13 << 20, transcendentals=0),
    )(order, src, pattern, own, scale, *pieces)


SIDE = 8
COLORS = 4


def at(a, b, core):
    a, b = a % SIDE, b % SIDE
    return (a * SIDE + b) * 2 if core == 0 else (b * SIDE + a) * 2 + 1


def places():
    return [(a, b, c) for c in range(2) for a in range(SIDE) for b in range(SIDE)]


def of_color(color, core):
    return [
        at(a, b, core)
        for a in range(SIDE)
        for b in range(SIDE)
        if (a + 2 * b) % COLORS == color
    ]


def arrival_order():
    table = np.zeros((2 * SIDE * SIDE, 2 * SIDE * SIDE), np.int32)
    for y in range(SIDE):
        for z in range(SIDE):
            for core in range(2):
                line = []
                for kind in (core, 1 - core):
                    a, b = (y, z) if kind == 0 else (z, y)
                    for turn in (0, 1, 3, 2):
                        line += of_color((a + 2 * b + turn) % COLORS, kind)
                table[(y * SIDE + z) * 2 + core] = line
    return table


def gather_pieces(rows):
    groups = [of_color(color, core) for core in range(2) for color in range(COLORS)]
    copies = jnp.broadcast_to(rows[None], (len(groups[0]),) + rows.shape)
    mine = lax.all_to_all(
        copies, "wide", split_axis=0, concat_axis=0, tiled=True, axis_index_groups=groups
    ).reshape(-1, rows.shape[1])
    half = mine.shape[0] // 2

    def taken(value, da, db):
        pairs = [(at(a + da, b + db, c), at(a, b, c)) for a, b, c in places()]
        return lax.ppermute(value, "wide", pairs)

    pieces = [
        mine,
        taken(mine, 1, 0),
        taken(mine, -1, 0),
        taken(mine[:half], 0, 1),
        taken(mine[half:], 0, -1),
    ]
    partner = [(i, i ^ 1) for i in range(2 * SIDE * SIDE)]
    return pieces + [lax.ppermute(piece, "wide", partner) for piece in pieces]


def on_device(
    grad_out,
    relu_mask,
    features,
    hop1_mean,
    hop2_mean,
    w_self,
    w_hop1,
    w_hop2,
    norm,
    tile_src,
    tile_owner,
    tile_block,
    tile_cols,
):
    gated = grad_out * relu_mask.astype(jnp.bfloat16)
    gated_full = lax.all_gather(gated, "narrow", axis=1, tiled=True)
    row_scale = norm[:, None]

    def project(weight):
        return lax.dot_general(
            gated_full, weight, (((1,), (1,)), ((), ())), preferred_element_type=jnp.float32
        )

    scaled2 = (row_scale * project(w_hop2)).astype(jnp.bfloat16)
    scaled2, tile_owner, gated_later = lax.optimization_barrier((scaled2, tile_owner, gated_full))
    rows2 = lax.all_gather(scaled2, "wide", axis=0, tiled=True)
    outgoing = route(tile_owner, tile_src, tile_block, jnp.swapaxes(tile_cols, 1, 2))
    arrived = lax.all_to_all(outgoing, "wide", split_axis=0, concat_axis=0, tiled=True)
    source = arrived[:, NNZ, 0].astype(jnp.int32)
    block = arrived[:, NNZ + 1, 0].astype(jnp.int32)
    order = lax.dynamic_index_in_dim(
        jnp.asarray(arrival_order()), lax.axis_index("wide"), 0, keepdims=False
    )
    pattern = build_pattern(order, block, arrived)
    partial_grads = jnp.stack(
        [
            jnp.einsum("ro,rd->od", gated_later, operand, preferred_element_type=jnp.float32)
            for operand in (features, hop1_mean, hop2_mean)
        ]
    )
    count = lax.axis_size("wide")
    kinds, outs, width = partial_grads.shape
    spread = lax.all_to_all(
        partial_grads.reshape(kinds, count, outs // count, width),
        "wide",
        split_axis=1,
        concat_axis=1,
        tiled=True,
    )
    weight_grads = spread.sum(axis=1)
    own1 = project(w_hop1)
    own0 = project(w_self)
    scaled1 = hop(order, source, pattern, own1, row_scale, [rows2], True)
    scaled1, weight_grads, own0 = lax.optimization_barrier((scaled1, weight_grads, own0))
    pieces = gather_pieces(scaled1)
    grad_features = hop(order, source, pattern, own0, jnp.ones_like(row_scale), pieces, False)
    return (grad_features, weight_grads)


def solution(mesh):
    placed = (
        P("wide", "narrow"),
        P("wide", "narrow"),
        P("wide", "narrow"),
        P("wide", "narrow"),
        P("wide", "narrow"),
        P("narrow", None),
        P("narrow", None),
        P("narrow", None),
        P("wide"),
        P("wide"),
        P("wide"),
        P("wide"),
        P("wide", None, None),
    )
    return jax.shard_map(
        on_device,
        mesh=mesh,
        in_specs=placed,
        out_specs=(P("wide", "narrow"), P(None, "wide", "narrow")),
        check_vma=False,
    )
```

```python
import functools

import jax
import jax.numpy as jnp
import numpy as np
from jax import lax
from jax.experimental import pallas as pl
from jax.experimental.pallas import tpu as pltpu
from jax.sharding import PartitionSpec as P

ROWS = 128
NNZ = 8
PACK = 16
KINDS = 3
LIMIT = 10 << 20


def route_kernel(owner_ref, src_ref, block_ref, cols_ref, out_ref):
    row = lax.broadcasted_iota(jnp.int32, (NNZ, ROWS), 0)

    def step(t, carry):
        cols = cols_ref[t]
        marks = jnp.where(row == 0, src_ref[t], jnp.where(row == 1, block_ref[t], 0))
        both = jnp.concatenate([cols, marks], axis=0).astype(jnp.float32)
        out_ref[owner_ref[t]] = both.astype(jnp.bfloat16)
        return carry

    lax.fori_loop(0, cols_ref.shape[0], step, 0, unroll=8)


def in_vmem(count):
    return [pl.BlockSpec(memory_space=pltpu.VMEM)] * count


def in_smem(count):
    return [pl.BlockSpec(memory_space=pltpu.SMEM)] * count


def route(tile_owner, tile_src, tile_block, cols):
    tiles = cols.shape[0]
    return pl.pallas_call(
        route_kernel,
        out_shape=jax.ShapeDtypeStruct((tiles, 2 * NNZ, ROWS), jnp.bfloat16),
        in_specs=in_smem(3) + in_vmem(1),
        out_specs=pl.BlockSpec(memory_space=pltpu.VMEM),
        compiler_params=pltpu.CompilerParams(vmem_limit_bytes=LIMIT),
        cost_estimate=pl.CostEstimate(flops=1 << 20, bytes_accessed=1 << 20, transcendentals=0),
    )(tile_owner, tile_src, tile_block, cols)


def pattern_kernel(order_ref, block_ref, cols_ref, out_ref):
    shape = (ROWS // PACK, PACK, ROWS)
    position = lax.broadcasted_iota(jnp.int32, shape, 0) * PACK
    position = position + lax.broadcasted_iota(jnp.int32, shape, 1)
    position = position.astype(jnp.float32).astype(jnp.bfloat16)
    one = jnp.ones(shape, jnp.bfloat16)
    zero = jnp.zeros(shape, jnp.bfloat16)

    def step(slot, carry):
        device = order_ref[slot]
        cols = cols_ref[device].astype(jnp.float32)
        count = zero
        for k in range(NNZ):
            line = jnp.broadcast_to(cols[k : k + 1, :], (PACK, ROWS)).astype(jnp.bfloat16)
            count = count + jnp.where(line[None] == position, one, zero)
        low = block_ref[device] == 0
        lanes = pl.ds(pl.multiple_of(slot * ROWS, ROWS), ROWS)
        out_ref[0:ROWS, lanes] = jnp.where(low, count, zero).reshape(ROWS, ROWS)
        out_ref[ROWS : 2 * ROWS, lanes] = jnp.where(low, zero, count).reshape(ROWS, ROWS)
        return carry

    lax.fori_loop(0, cols_ref.shape[0], step, 0, unroll=8)


def build_pattern(order, block, arrived):
    tiles = arrived.shape[0]
    return pl.pallas_call(
        pattern_kernel,
        out_shape=jax.ShapeDtypeStruct((2 * ROWS, tiles * ROWS), jnp.bfloat16),
        in_specs=in_smem(2) + in_vmem(1),
        out_specs=pl.BlockSpec(memory_space=pltpu.VMEM),
        compiler_params=pltpu.CompilerParams(vmem_limit_bytes=LIMIT),
        cost_estimate=pl.CostEstimate(flops=1 << 26, bytes_accessed=9 << 20, transcendentals=0),
    )(order, block, arrived)


def product(order_ref, src_ref, pattern_ref, rows_ref, slot):
    held = rows_ref.shape[0] // (2 * ROWS)
    picked = []
    for i in range(held):
        start = pl.multiple_of((2 * i + src_ref[order_ref[slot + i]]) * ROWS, ROWS)
        picked.append(rows_ref[pl.ds(start, ROWS), :])
    return jnp.dot(
        pattern_ref[:, slot * ROWS : (slot + held) * ROWS],
        jnp.concatenate(picked, axis=0),
        preferred_element_type=jnp.float32,
    )


def total_of(order_ref, src_ref, pattern_ref, own_ref, pieces):
    total = own_ref[...]
    slot = 0
    for rows in pieces:
        total = total + product(order_ref, src_ref, pattern_ref, rows, slot)
        slot += rows.shape[0] // (2 * ROWS)
    return total


def hop_kernel(order_ref, src_ref, pattern_ref, own_ref, scale_ref, extra_ref, *rest):
    total = total_of(order_ref, src_ref, pattern_ref, own_ref, rest[:-1])
    scaled = (scale_ref[...] * total).astype(jnp.bfloat16)
    nodes = scaled.shape[0]
    for peer in range(extra_ref.shape[0]):
        rest[-1][peer, 0:nodes, :] = scaled
        rest[-1][peer, nodes:, :] = extra_ref[peer]


def last_hop_kernel(order_ref, src_ref, pattern_ref, own_ref, spread_ref, *rest):
    rows_out, grads_out = rest[-2:]
    total = total_of(order_ref, src_ref, pattern_ref, own_ref, rest[:-2])
    rows_out[...] = total.astype(jnp.bfloat16)
    grads = spread_ref[...].astype(jnp.float32).sum(axis=0)
    grads = grads[0:PACK] + grads[PACK : 2 * PACK]
    kinds, outs, _ = grads_out.shape
    for kind in range(kinds):
        grads_out[kind] = grads[kind * outs : (kind + 1) * outs]


def run_hop(kernel, outs, order, src, held):
    return pl.pallas_call(
        kernel,
        out_shape=outs,
        in_specs=in_smem(2) + in_vmem(len(held)),
        out_specs=jax.tree.map(lambda _: pl.BlockSpec(memory_space=pltpu.VMEM), outs),
        compiler_params=pltpu.CompilerParams(vmem_limit_bytes=LIMIT),
        cost_estimate=pl.CostEstimate(flops=1 << 30, bytes_accessed=13 << 20, transcendentals=0),
    )(order, src, *held)


def hop(order, src, pattern, own, scale, extra, pieces):
    peers, more, width = extra.shape
    sent = jax.ShapeDtypeStruct((peers, own.shape[0] + more, width), jnp.bfloat16)
    return run_hop(hop_kernel, sent, order, src, [pattern, own, scale, extra] + pieces)


def last_hop(order, src, pattern, own, spread, pieces):
    outs = (
        jax.ShapeDtypeStruct(own.shape, jnp.bfloat16),
        jax.ShapeDtypeStruct((KINDS, spread.shape[0] // COLORS, own.shape[1]), jnp.float32),
    )
    return run_hop(last_hop_kernel, outs, order, src, [pattern, own, spread] + pieces)


SIDE = 8
COLORS = 4


def at(a, b, core):
    a, b = a % SIDE, b % SIDE
    return (a * SIDE + b) * 2 if core == 0 else (b * SIDE + a) * 2 + 1


def places():
    return [(a, b, c) for c in range(2) for a in range(SIDE) for b in range(SIDE)]


def of_color(color, core):
    return [
        at(a, b, core)
        for a in range(SIDE)
        for b in range(SIDE)
        if (a + 2 * b) % COLORS == color
    ]


def arrival_order():
    table = np.zeros((2 * SIDE * SIDE, 2 * SIDE * SIDE), np.int32)
    for y in range(SIDE):
        for z in range(SIDE):
            for core in range(2):
                line = []
                for kind in (core, 1 - core):
                    a, b = (y, z) if kind == 0 else (z, y)
                    for turn in (0, 1, 3, 2):
                        line += of_color((a + 2 * b + turn) % COLORS, kind)
                table[(y * SIDE + z) * 2 + core] = line
    return table


def color_groups():
    return [of_color(color, core) for core in range(2) for color in range(COLORS)]


def taken(value, da, db):
    pairs = [(at(a + da, b + db, c), at(a, b, c)) for a, b, c in places()]
    return lax.ppermute(value, "wide", pairs)


def from_partner(value):
    return lax.ppermute(value, "wide", [(i, i ^ 1) for i in range(2 * SIDE * SIDE)])


def among_color(sent):
    return lax.all_to_all(
        sent, "wide", split_axis=0, concat_axis=0, tiled=True, axis_index_groups=color_groups()
    )


def near_pieces(mine):
    half = mine.shape[0] // 2
    return [taken(mine, 1, 0), taken(mine, -1, 0), taken(mine[:half], 0, 1), taken(mine[half:], 0, -1)]


def color_sums(gated_full, order, operands):
    outs = gated_full.shape[1] // order.shape[0]
    wanted = (order[:, None] * outs + jnp.arange(outs, dtype=jnp.int32)[None]).reshape(-1)
    pick = (jnp.arange(gated_full.shape[1], dtype=jnp.int32)[:, None] == wanted[None]).astype(jnp.bfloat16)
    sorted_gated = jnp.dot(gated_full, pick, preferred_element_type=jnp.float32).astype(jnp.bfloat16)
    partial = jnp.stack(
        [
            jnp.einsum("ro,rd->od", sorted_gated, operand, preferred_element_type=jnp.float32)
            for operand in operands
        ]
    )
    half = partial.shape[1] // 2
    kept = partial[:, :half] + from_partner(partial[:, half:])
    part = half // COLORS
    parts = [kept[:, i * part : (i + 1) * part] for i in range(COLORS)]
    summed = parts[0] + taken(parts[1], -1, 0) + taken(parts[2], 1, 0) + taken(parts[3], 0, -1)
    kinds, _, width = summed.shape
    peers = part // outs
    summed = jnp.swapaxes(summed.reshape(kinds, peers, outs, width), 0, 1)
    summed = summed.reshape(peers, kinds * outs, width)
    summed = jnp.pad(summed, ((0, 0), (0, PACK - kinds * outs), (0, 0)))
    high = lax.reduce_precision(summed, 8, 7)
    return jnp.concatenate([high, summed - high], axis=1).astype(jnp.bfloat16)


def on_device(
    grad_out,
    relu_mask,
    features,
    hop1_mean,
    hop2_mean,
    w_self,
    w_hop1,
    w_hop2,
    norm,
    tile_src,
    tile_owner,
    tile_block,
    tile_cols,
):
    outgoing = route(tile_owner, tile_src, tile_block, jnp.swapaxes(tile_cols, 1, 2))
    arrived = lax.all_to_all(outgoing, "wide", split_axis=0, concat_axis=0, tiled=True)
    gated = grad_out * relu_mask.astype(jnp.bfloat16)
    gated_full = lax.all_gather(gated, "narrow", axis=1, tiled=True)
    row_scale = norm[:, None]

    def project(weight):
        return lax.dot_general(
            gated_full, weight, (((1,), (1,)), ((), ())), preferred_element_type=jnp.float32
        )

    scaled2 = (row_scale * project(w_hop2)).astype(jnp.bfloat16)
    scaled2, arrived, gated_full = lax.optimization_barrier((scaled2, arrived, gated_full))
    peers = len(color_groups()[0])
    nodes, width = scaled2.shape
    mine = among_color(jnp.broadcast_to(scaled2[None], (peers, nodes, width)))
    source = arrived[:, NNZ, 0].astype(jnp.int32)
    block = arrived[:, NNZ + 1, 0].astype(jnp.int32)
    order = lax.dynamic_index_in_dim(
        jnp.asarray(arrival_order()), lax.axis_index("wide"), 0, keepdims=False
    )
    extra = color_sums(gated_full, order, (features, hop1_mean, hop2_mean))
    beside = (source, block, order, arrived, extra, project(w_hop1), project(w_self))
    beside += (jnp.broadcast_to(row_scale, (nodes, width)),)
    mine, beside = lax.optimization_barrier((mine, beside))
    source, block, order, arrived, extra, own1, own0, wide_scale = beside
    mine = mine.reshape(peers * nodes, width)
    mine_far = from_partner(mine)
    near = near_pieces(mine)
    pattern = build_pattern(order, block, arrived)
    near[0], pattern = lax.optimization_barrier((near[0], pattern))
    pieces = [mine] + near + [mine_far] + [from_partner(piece) for piece in near]
    sent = hop(order, source, pattern, own1, wide_scale, extra, pieces)
    got = among_color(sent)
    mine = got[:, :nodes].reshape(peers * nodes, width)
    near = near_pieces(mine)
    pieces = [mine] + near + [from_partner(piece) for piece in [mine] + near]
    grad_features, weight_grads = last_hop(order, source, pattern, own0, got[:, nodes:], pieces)
    return (grad_features, weight_grads)


def solution(mesh):
    placed = (
        P("wide", "narrow"),
        P("wide", "narrow"),
        P("wide", "narrow"),
        P("wide", "narrow"),
        P("wide", "narrow"),
        P("narrow", None),
        P("narrow", None),
        P("narrow", None),
        P("wide"),
        P("wide"),
        P("wide"),
        P("wide"),
        P("wide", None, None),
    )
    return jax.shard_map(
        on_device,
        mesh=mesh,
        in_specs=placed,
        out_specs=(P("wide", "narrow"), P(None, "wide", "narrow")),
        check_vma=False,
    )
```
